32 devices in a mesh: row: 4 (over x, core), col: 8 (over z, y).
Axes of the slice: x: 2, y: 2, z: 4, core: 2. Of those that a mesh axis runs over, the one named last changes fastest.
Arguments:
- hidden: bfloat16 [128, 8192], P('row', 'col'), may hold values from -6 to 6
- vectors: float32 [4, 8192], P(None, 'col'), may hold values from -6 to 6
- gain: float32 [8192], P('col'), may hold values from 0.25 to 1.75
- lengths: int32 [2], replicated, may hold values from 16 to 64, as said below
- gate_weight: bfloat16 [8192, 29568], P('col', 'row'), may hold values from -0.0625 to 0.0625
- up_weight: bfloat16 [8192, 29568], P('col', 'row'), may hold values from -0.0625 to 0.0625
- down_weight: bfloat16 [29568, 8192], P('row', 'col'), may hold values from -0.03125 to 0.03125
Outputs:
- output: bfloat16 [128, 8192], P('row', 'col')
- tangent_out: bfloat16 [128, 4, 8192], P('row', None, 'col')
- new_vectors: float32 [4, 8192], P(None, 'col')
- back_cross: float32 [128, 4], P('row')
The draws below stay inside these ranges and needn't reach their ends.
Inputs may be any that keep to these rules, and one draw needn't show every extreme that they name: `lengths`: each prompt's live tokens come first; in every draw exactly one prompt has all 64 tokens live.
All inputs are finite; a program needn't handle non-finite values.
Results may differ from the reference program's by a relative error of at most 0.025.
Values may be sent and summed in bfloat16 or wider, within the bound.
No kernel may reach another device: no remote copies, remote signals or barrier semaphores. Data moves between devices by JAX's collectives and lax.ppermute only.
A program may use at most 192 MiB of HBM per device.

```python
import jax
import jax.numpy as jnp
from jax import lax

D = 8192
FF = 29568
CANDIDATES = 4
PROMPTS = 2
LEN = 64
TOKENS = 128
N_COL = 8


def draw_lengths(key, part):
    first_key, second_key = jax.random.split(jax.random.fold_in(key, 17))
    drawn = jax.random.randint(first_key, (PROMPTS,), LEN // 4, LEN)
    filled = jax.random.randint(second_key, (), 0, PROMPTS)
    return jnp.where(jnp.arange(PROMPTS) == filled, LEN, drawn).astype(jnp.int32)


def level_of(rng, extent, cuts, least, largest):
    factor_of, own = 1.0, jax.random.fold_in(rng, 6)
    for axis_at, blocks in cuts:
        heights = jnp.exp(jax.random.uniform(jax.random.fold_in(own, axis_at), (blocks,), jnp.float32, least / len(cuts), largest / len(cuts)))
        factor_of = factor_of * jnp.repeat(heights, extent[axis_at] // blocks).reshape([-1 if axis == axis_at else 1 for axis in range(len(extent))])
    return factor_of


def scatter_about(key, extent, spread, most, cuts=(), kind=jnp.bfloat16):
    array = spread * jax.random.normal(key, extent, jnp.float32)
    if cuts:
        array = array * level_of(key, extent, cuts, -0.22, 0.18)
    return jnp.clip(array, -most, most).astype(kind)


def setup_inputs(seed: int = 0) -> dict:
    arg_keys = jax.random.split(jax.random.key(seed), 8)
    hidden = scatter_about(arg_keys[0], (TOKENS, D), 1.0, 6.0, ((0, 4), (1, 8)))
    vectors = scatter_about(arg_keys[1], (CANDIDATES, D), 1.0, 6.0, ((1, 8),), jnp.float32)
    gain = jnp.clip(1.0 + 0.15 * jax.random.normal(arg_keys[2], (D,), jnp.float32), 0.25, 1.75)
    lengths = draw_lengths(jax.random.fold_in(arg_keys[7], 71), 0)
    gate_weight = scatter_about(arg_keys[4], (D, FF), D ** -0.5, 0.0625, ((0, 8), (1, 4)))
    up_weight = scatter_about(arg_keys[5], (D, FF), D ** -0.5, 0.0625, ((0, 8), (1, 4)))
    down_weight = scatter_about(arg_keys[6], (FF, D), FF ** -0.5, 0.03125, ((0, 4), (1, 8)))
    return {"hidden": hidden, "vectors": vectors, "gain": gain, "lengths": lengths, "gate_weight": gate_weight, "up_weight": up_weight, "down_weight": down_weight}


EPSILON = 1e-06
HIGH = lax.Precision.HIGHEST

def silu_parts(value):
    sigmoid = jax.nn.sigmoid(value)
    return (value * sigmoid, sigmoid * (1.0 + value * (1.0 - sigmoid)))

def contract(left, right, left_dim, right_dim):
    return lax.dot_general(left.astype(jnp.float32), right.astype(jnp.float32), (((left_dim,), (right_dim,)), ((), ())), preferred_element_type=jnp.float32)

def blocked(left, right, right_dim):
    width = left.shape[1] // N_COL
    total = None
    for block in range(N_COL):
        left_part = lax.slice_in_dim(left, block * width, (block + 1) * width, axis=1)
        right_part = lax.slice_in_dim(right, block * width, (block + 1) * width, axis=right_dim)
        term = contract(left_part, right_part, 1, right_dim)
        term = lax.optimization_barrier(term.astype(jnp.bfloat16)).astype(jnp.float32)
        total = term if total is None else total + term
    return total

def reference(hidden, vectors, gain, lengths, gate_weight, up_weight, down_weight):
    hidden_f = hidden.astype(jnp.float32)
    tokens = hidden.shape[0]
    count = vectors.shape[0]
    width_s = count + 1
    square = lax.optimization_barrier(jnp.sum(hidden_f * hidden_f, axis=1))
    rscale = lax.rsqrt(square / D + EPSILON)
    cross = jnp.dot(hidden_f, vectors.T, precision=HIGH)
    primal = hidden_f * rscale[:, None] * gain
    tangent = (vectors[None] * rscale[:, None, None] - hidden_f[:, None, :] * (rscale ** 3)[:, None, None] * (cross / D)[:, :, None]) * gain
    streams = jnp.concatenate([primal[:, None], tangent], axis=1).astype(jnp.bfloat16)
    flat = streams.reshape(tokens * width_s, D)
    gate = blocked(flat, gate_weight, 0).reshape(tokens, width_s, FF)
    up = blocked(flat, up_weight, 0).reshape(tokens, width_s, FF)
    act, slope = silu_parts(gate[:, 0])
    up_primal = up[:, 0]
    tangent_hidden = slope[:, None] * gate[:, 1:] * up_primal[:, None] + act[:, None] * up[:, 1:]
    hidden_act = jnp.concatenate([(act * up_primal)[:, None], tangent_hidden], axis=1).astype(jnp.bfloat16)
    down = jnp.dot(hidden_act.reshape(tokens * width_s, FF).astype(jnp.float32), down_weight.astype(jnp.float32), preferred_element_type=jnp.float32).reshape(tokens, width_s, D)
    output = (hidden_f + down[:, 0]).astype(jnp.bfloat16)
    tangent_out = (vectors[None] + down[:, 1:]).astype(jnp.bfloat16)
    position = lax.iota(jnp.int32, tokens)
    prompt = position // LEN
    limit = lengths[prompt]
    live = (position % LEN < limit).astype(jnp.bfloat16)
    cotangent = tangent_out * live[:, None, None]
    back_hidden = blocked(cotangent.reshape(tokens * count, D), down_weight, 1).reshape(tokens, count, FF)
    back_gate = (back_hidden * up_primal[:, None] * slope[:, None]).astype(jnp.bfloat16)
    back_up = (back_hidden * act[:, None]).astype(jnp.bfloat16)
    back_normed = (contract(back_gate.reshape(tokens * count, FF), gate_weight, 1, 1) + contract(back_up.reshape(tokens * count, FF), up_weight, 1, 1)).reshape(tokens, count, D)
    scaled = back_normed * gain
    back_cross = lax.optimization_barrier(jnp.sum(scaled * hidden_f[:, None], axis=2))
    grad = cotangent.astype(jnp.float32) + scaled * rscale[:, None, None] - hidden_f[:, None] * (rscale ** 3)[:, None, None] * (back_cross / D)[:, :, None]
    total = lax.optimization_barrier(jnp.sum(grad, axis=0))
    gram = jnp.dot(total, total.T, precision=HIGH)
    lower = jnp.linalg.cholesky(gram)
    new_vectors = lax.linalg.triangular_solve(lower, total, left_side=True, lower=True) * D ** 0.5
    return (output, tangent_out, new_vectors, back_cross)
```

```python
import jax
import jax.numpy as jnp
from jax import lax
from jax.sharding import PartitionSpec as P

D = 8192
LEN = 64


EPSILON = 1e-06
HIGH = lax.Precision.HIGHEST


def silu_parts(value):
    sigmoid = jax.nn.sigmoid(value)
    return (value * sigmoid, sigmoid * (1.0 + value * (1.0 - sigmoid)))


def contract(left, right, left_dim, right_dim):
    return lax.dot_general(
        left, right, (((left_dim,), (right_dim,)), ((), ())), preferred_element_type=jnp.float32
    )


def per_device(hidden, vectors, gain, lengths, gate_weight, up_weight, down_weight):
    rows = hidden.shape[0]
    width = hidden.shape[1]
    count = vectors.shape[0]
    tokens = rows * lax.axis_size("row")
    hidden_all = lax.all_gather(hidden, "row", axis=0, tiled=True)
    hidden_f = hidden_all.astype(jnp.float32)
    sums = lax.psum(
        jnp.concatenate(
            [
                jnp.sum(hidden_f * hidden_f, axis=1)[:, None],
                jnp.dot(hidden_f, vectors.T, precision=HIGH),
            ],
            axis=1,
        ),
        "col",
    )
    rscale = lax.rsqrt(sums[:, 0] / D + EPSILON)
    mix = (rscale**2)[:, None] * sums[:, 1:] / D
    piece = jnp.concatenate([hidden_f * gain, vectors * gain], axis=0).astype(jnp.bfloat16)
    gate_part = jnp.dot(piece, gate_weight, preferred_element_type=jnp.float32)
    up_part = jnp.dot(piece, up_weight, preferred_element_type=jnp.float32)
    gate_up = lax.psum(
        jnp.concatenate([gate_part.astype(jnp.bfloat16), up_part.astype(jnp.bfloat16)], axis=0),
        "col",
    ).astype(jnp.float32)
    high = tokens + count
    gate_raw = gate_up[:tokens]
    gate_vec = gate_up[tokens:high]
    up_raw = gate_up[high : high + tokens]
    up_vec = gate_up[high + tokens :]
    gate = gate_raw * rscale[:, None]
    up = up_raw * rscale[:, None]
    act, slope = silu_parts(gate)
    slope_up = slope * up
    scaled_act = act * rscale[:, None]
    scaled_slope = slope_up * rscale[:, None]
    both = slope_up * gate + act * up
    tangent_hidden = (
        scaled_slope[None] * gate_vec[:, None]
        + scaled_act[None] * up_vec[:, None]
        - mix.T[:, :, None] * both[None]
    )
    hidden_act = jnp.concatenate([(act * up)[None], tangent_hidden], axis=0).astype(jnp.bfloat16)
    down = lax.psum_scatter(
        jnp.dot(
            hidden_act.reshape((count + 1) * tokens, -1),
            down_weight,
            preferred_element_type=jnp.float32,
        )
        .reshape(count + 1, tokens, width)
        .astype(jnp.bfloat16),
        "row",
        scatter_dimension=1,
        tiled=True,
    ).astype(jnp.float32)
    output = (hidden.astype(jnp.float32) + down[0]).astype(jnp.bfloat16)
    tangent = (vectors[:, None] + down[1:]).astype(jnp.bfloat16)
    start = lax.axis_index("row") * rows
    position = start + lax.iota(jnp.int32, rows)
    prompt = position // LEN
    limit = jnp.sum(
        jnp.where(
            prompt[:, None] == lax.iota(jnp.int32, lengths.shape[0])[None, :], lengths[None, :], 0
        ),
        axis=1,
    )
    live = (position % LEN < limit).astype(jnp.bfloat16)
    cotangent = tangent * live[None, :, None]
    cot_all = lax.all_gather(cotangent, "row", axis=1, tiled=True)
    product = contract(cot_all.reshape(count * tokens, width), down_weight, 1, 1).reshape(
        count, tokens, -1
    )
    gate_sum = jnp.sum(product * scaled_slope[None], axis=1)
    up_sum = jnp.sum(product * scaled_act[None], axis=1)
    weight = slope_up * gate_raw + act * up_raw
    cross_part = jnp.sum(product * weight[None], axis=2)
    gate_sum, up_sum, cross_part = lax.psum((gate_sum, up_sum, cross_part), "col")
    pulled = gain * (
        contract(gate_sum.astype(jnp.bfloat16), gate_weight, 1, 1)
        + contract(up_sum.astype(jnp.bfloat16), up_weight, 1, 1)
    )
    shift = jnp.dot(cross_part * (rscale**3 / D)[None, :], hidden_f, precision=HIGH)
    partial = jnp.sum(cotangent.astype(jnp.float32), axis=1) + pulled - shift
    total, back_cross = lax.psum((partial, cross_part), "row")
    gram = lax.psum(jnp.dot(total, total.T, precision=HIGH), "col")
    lower = jnp.linalg.cholesky(gram)
    new_vectors = lax.linalg.triangular_solve(lower, total, left_side=True, lower=True) * D**0.5
    own_cross = lax.dynamic_slice_in_dim(back_cross, start, rows, axis=1).T
    return (output, jnp.transpose(tangent, (1, 0, 2)), new_vectors, own_cross)


def solution(mesh):
    return jax.shard_map(
        per_device,
        mesh=mesh,
        in_specs=(
            P("row", "col"),
            P(None, "col"),
            P("col"),
            P(),
            P("col", "row"),
            P("col", "row"),
            P("row", "col"),
        ),
        out_specs=(P("row", "col"), P("row", None, "col"), P(None, "col"), P("row", None)),
        check_vma=False,
    )
```

```python
import functools

import jax
import jax.numpy as jnp
from jax import lax
from jax.experimental import pallas as pl
from jax.experimental.pallas import tpu as pltpu
from jax.sharding import PartitionSpec as P

D = 8192
LEN = 64


EPSILON = 1e-06
HIGH = lax.Precision.HIGHEST
BLOCK = 896
BF16 = jnp.bfloat16
F32 = jnp.float32


def silu_parts(value):
    sigmoid = jax.nn.sigmoid(value)
    return (value * sigmoid, sigmoid * (1.0 + value * (1.0 - sigmoid)))


def contract(left, right, left_dim, right_dim):
    return lax.dot_general(
        left, right, (((left_dim,), (right_dim,)), ((), ())), preferred_element_type=jnp.float32
    )


def exchange(value, axis, mask):
    size = lax.axis_size(axis)
    return lax.ppermute(value, axis, [(i, i ^ mask) for i in range(size)])


def doubling(value, axis, send=None):
    mask = 1
    while mask < lax.axis_size(axis):
        if send is None:
            value = jax.tree.map(lambda v: v + exchange(v, axis, mask), value)
        else:
            own = value.astype(send)
            value = own.astype(F32) + exchange(own, axis, mask).astype(F32)
        mask *= 2
    return value


def starts(units):
    return [(begin, min(BLOCK, units - begin)) for begin in range(0, units, BLOCK)]


def fetch(sources, copies, arrived):
    def copy(which, block, begin, size):
        rows = pl.ds(begin, size)
        return pltpu.make_async_copy(
            sources[which].at[rows], copies[which].at[rows], arrived.at[which, block]
        )

    blocks = starts(sources[0].shape[0])
    step = pl.program_id(0)

    @pl.when(step == 0)
    def _():
        for block, place in enumerate(blocks):
            for which in range(len(sources)):
                copy(which, block, *place).start()

    def wait(block, last=False):
        for which in range(len(sources)):
            if last:
                copy(which, len(blocks) - 1, *blocks[-1]).wait()
            else:
                copy(which, block, pl.multiple_of(block * BLOCK, BLOCK), BLOCK).wait()

    return wait


def store(weights):
    units, width = weights[0].shape
    return [pltpu.VMEM((units, width), BF16) for _ in weights] + [
        pltpu.SemaphoreType.DMA((len(weights), pl.cdiv(units, BLOCK)))
    ]


def products_kernel(first, x_ref, gate_hbm, up_hbm, *refs):
    outs = (refs[0:2], refs[2:4])
    vec_ref, *weights, arrived = refs[4:]
    wait = fetch((gate_hbm, up_hbm), weights, arrived)
    step = pl.program_id(0)
    chunks, per, _ = outs[0][0].shape
    count = vec_ref.shape[1]
    tokens = chunks * per
    units = vec_ref.shape[2]
    full = units // BLOCK

    def put(part, begin, size):
        at = pl.ds(pl.multiple_of((step - begin) * BLOCK, 128), size)
        to = pl.ds(pl.multiple_of(step * BLOCK, 128), size)
        for index in range(2):
            weight = weights[index][pl.ds(pl.multiple_of(step * BLOCK, BLOCK), size)]
            result = contract(weight, x_ref[...], 1, 1).T
            outs[part][index][:, :, at] = result[:tokens].reshape(chunks, per, size).astype(BF16)
            vec_ref[index, :, to] = result[tokens : tokens + count] + result[tokens + count :]

    pl.when(step < full)(lambda: wait(step))
    pl.when(step == full)(lambda: wait(step, True))
    pl.when(step < first)(lambda: put(0, 0, BLOCK))
    pl.when(jnp.logical_and(step >= first, step < full))(lambda: put(1, first, BLOCK))
    pl.when(step == full)(lambda: put(1, first, units - full * BLOCK))


def products(x, gate_turned, up_turned, chunks, per, count, first):
    units, depth = gate_turned.shape
    resident = pl.BlockSpec(memory_space=pltpu.VMEM)
    anywhere = pl.BlockSpec(memory_space=pltpu.HBM)
    part = lambda width: jax.ShapeDtypeStruct((chunks, per, width), BF16)
    widths = (first * BLOCK, units - first * BLOCK)
    *mains, vec = pl.pallas_call(
        functools.partial(products_kernel, first),
        grid=(units // BLOCK + 1,),
        in_specs=[resident, anywhere, anywhere],
        out_specs=[resident] * 5,
        out_shape=[part(width) for width in widths for _ in range(2)]
        + [jax.ShapeDtypeStruct((2, count, units), F32)],
        scratch_shapes=store((gate_turned, up_turned)),
        compiler_params=pltpu.CompilerParams(vmem_limit_bytes=52 << 20),
        cost_estimate=pl.CostEstimate(
            flops=4 * x.shape[0] * depth * units,
            bytes_accessed=4 * depth * units,
            transcendentals=0,
        ),
        name="products",
    )(x, gate_turned, up_turned)
    return [mains[:2], mains[2:]], vec


def halves(value):
    high = value.astype(BF16)
    return [high, (value - high.astype(F32)).astype(BF16)]


def pack(rough, exact):
    return jnp.concatenate([rough.astype(BF16), *halves(exact)], axis=1)


def unpack(packed, width):
    wide = packed.astype(F32)
    size = (packed.shape[1] - width) // 2
    return wide[:, :width], wide[:, width : width + size] + wide[:, width + size :]


def ring_sum(mains, rough, exact):
    size = lax.axis_size("col")
    order = list(range(0, size, 2)) + list(range(1, size, 2))[::-1]
    column = lax.axis_index("col")
    place = jnp.where(column % 2 == 0, column // 2, size - 1 - column // 2)
    perms = (
        [(order[i], order[(i + 1) % size]) for i in range(size)],
        [(order[(i + 1) % size], order[i]) for i in range(size)],
    )
    signs = (-1, 1)
    streams = [(part, way) for part in range(len(mains)) for way in range(2)]

    def slot(way, offset):
        return (place + signs[way] * offset + size) % size

    def chunk(stream, offset):
        part, way = stream
        return lax.dynamic_index_in_dim(mains[part][way], slot(way, offset), 0, keepdims=False)

    flight = {"rough": rough, "exact": exact, "mask": 1, "count": 0}

    def side(mark):
        count = flight["count"]
        flight["count"] += 1
        if count < 4:
            return
        if (count - 4) % 3 == 0 and flight["mask"] < size:
            own, _ = lax.optimization_barrier((pack(flight["rough"], flight["exact"]), mark))
            flight["pair"] = (own, exchange(own, "col", flight["mask"]))
            flight["mask"] *= 2
        elif (count - 4) % 3 == 2 and "pair" in flight:
            own, other = flight.pop("pair")
            other, _ = lax.optimization_barrier((other, mark))
            width = rough.shape[1]
            mine, theirs = unpack(own, width), unpack(other, width)
            flight["rough"], flight["exact"] = (x + y for x, y in zip(mine, theirs))

    held = {s: chunk(s, 1) for s in streams}
    for step in range(size - 1):
        for s in streams:
            got = lax.ppermute(held[s], "col", perms[s[1]])
            held[s] = (got.astype(F32) + chunk(s, step + 2).astype(F32)).astype(BF16)
        side(held[streams[-1]])
    arrived = {s: [held[s]] for s in streams}
    for step in range(size - 1):
        for s in streams:
            arrived[s].append(lax.ppermute(arrived[s][-1], "col", perms[s[1]]))
        side(arrived[streams[-1]][-1])
    places = jnp.stack([slot(way, offset) for way in range(2) for offset in range(size)])
    return arrived, places.astype(jnp.int32), flight["rough"], flight["exact"]


def down_kernel(first, full, chunks, collecting, places, *refs):
    if collecting:
        arrived, refs = refs[: 4 * chunks], refs[4 * chunks :]
        vec_ref, rows_ref, hbm, out_ref, factor_ref, raw, held, acc, weight, ready = refs
    else:
        raw, vec_ref, rows_ref, hbm, out_ref, factor_ref, held, acc, weight, ready = refs
    step = pl.program_id(0)
    streams, tokens, width = out_ref.shape
    per = raw.shape[2]
    tail = weight.shape[0] - full * BLOCK
    wait = fetch((hbm,), (weight,), ready)
    group = max(1, 16 // per)
    half = places[2 * chunks] * (chunks // 2)

    def collect(part, at, to):
        for way in range(2):
            for index in range(chunks):
                piece = arrived[(2 * part + way) * chunks + index]
                raw[way, places[way * chunks + index], :, to] = piece[:, at]

    def lanes(block):
        return pl.ds(pl.multiple_of(block * BLOCK, 128), BLOCK)

    if collecting:

        @pl.when(step < first)
        def _():
            collect(0, lanes(step), lanes(step))

        @pl.when(jnp.logical_and(step >= first, step < full))
        def _():
            collect(1, lanes(step - first), lanes(step))

        @pl.when(step == full)
        def _():
            begin = (full - first) * BLOCK
            collect(1, slice(begin, begin + tail), slice(full * BLOCK, full * BLOCK + tail))

    def fill(slot, number, lane):
        size = group * per
        rows = slice(number * size, (number + 1) * size)
        chosen = pl.ds(half + number * group, group)
        here = slice(lane, lane + 128)
        at = pl.ds(pl.multiple_of(step * BLOCK + lane, 128), 128)
        gate_raw, up_raw = (
            raw[way, chosen, :, at].astype(F32).reshape(size, 128) for way in range(2)
        )
        scale = rows_ref[0, rows]
        gate = gate_raw * scale
        up = up_raw * scale
        act, slope = silu_parts(gate)
        slope_up = slope * up
        primal = act * up
        both = slope_up * gate + primal
        scaled_slope = slope_up * scale
        scaled_act = act * scale
        factor_ref[0, rows, at] = scaled_slope.astype(BF16)
        factor_ref[1, rows, at] = scaled_act.astype(BF16)
        factor_ref[2, rows, at] = (slope_up * gate_raw + act * up_raw).astype(BF16)
        held[slot, 0, rows, here] = primal.astype(BF16)
        for k in range(streams - 1):
            held[slot, k + 1, rows, here] = (
                scaled_slope * vec_ref[0, k : k + 1, here]
                + scaled_act * vec_ref[1, k : k + 1, here]
                - rows_ref[k + 1, rows] * both
            ).astype(BF16)

    def last():
        return held[1 - step % 2].reshape(streams * tokens, BLOCK)

    def fill_all():
        for number in range(tokens // (group * per)):
            for lane in range(0, BLOCK, 128):
                fill(step % 2, number, lane)

    @pl.when(step == 0)
    def _():
        acc[...] = jnp.zeros_like(acc)
        fill_all()

    @pl.when(jnp.logical_and(step >= 1, step <= full))
    def _():
        wait(step - 1)
        rows = pl.ds(pl.multiple_of((step - 1) * BLOCK, BLOCK), BLOCK)
        acc[...] += jnp.dot(last(), weight[rows], preferred_element_type=F32)
        fill_all()

    @pl.when(step == full + 1)
    def _():
        wait(full, True)
        rows = slice(full * BLOCK, full * BLOCK + tail)
        result = acc[...] + jnp.dot(last()[:, :tail], weight[rows], preferred_element_type=F32)
        out_ref[...] = result.reshape(streams, tokens, width).astype(BF16)


def down_product(source, shape, places, vec, row_values, weight, first):
    units, width = weight.shape
    full = units // BLOCK
    chunks, per = shape
    tokens = row_values.shape[1]
    count = vec.shape[1]
    resident = pl.BlockSpec(memory_space=pltpu.VMEM)
    padded = (full + 1) * BLOCK
    collecting = len(source) > 1
    return pl.pallas_call(
        functools.partial(down_kernel, first, full, chunks, collecting),
        grid_spec=pltpu.PrefetchScalarGridSpec(
            num_scalar_prefetch=1,
            grid=(full + 2,),
            in_specs=[resident] * len(source)
            + [
                pl.BlockSpec((2, count, BLOCK), lambda i, p: (0, 0, jnp.minimum(i, full))),
                resident,
                pl.BlockSpec(memory_space=pltpu.HBM),
            ],
            out_specs=[
                pl.BlockSpec((count + 1, tokens, width), lambda i, p: (0, 0, 0)),
                resident,
            ]
            + [resident] * collecting,
            scratch_shapes=[
                pltpu.VMEM((2, count + 1, tokens, BLOCK), BF16),
                pltpu.VMEM(((count + 1) * tokens, width), F32),
                *store((weight,)),
            ],
        ),
        out_shape=[
            jax.ShapeDtypeStruct((count + 1, tokens, width), BF16),
            jax.ShapeDtypeStruct((3, tokens, padded), BF16),
        ]
        + [jax.ShapeDtypeStruct((2, chunks, per, padded), BF16)] * collecting,
        compiler_params=pltpu.CompilerParams(vmem_limit_bytes=(50 if collecting else 50) << 20),
        cost_estimate=pl.CostEstimate(
            flops=2 * (count + 1) * tokens * units * width,
            bytes_accessed=2 * units * width,
            transcendentals=tokens * units,
        ),
        name="down_product",
    )(places, *source, vec, row_values, weight)


def back_kernel(units, factor_ref, cot_ref, hbm, sum_ref, cross_ref, cross, weight, ready):
    step = pl.program_id(0)
    tokens = factor_ref.shape[1]
    count = cot_ref.shape[0] // tokens
    base = step * BLOCK

    @pl.when(step == 0)
    def _():
        cross[...] = jnp.zeros_like(cross)

    full = units // BLOCK
    wait = fetch((hbm,), (weight,), ready)
    pl.when(step < full)(lambda: wait(step))
    pl.when(step == full)(lambda: wait(step, True))

    def part(begin, end):
        rows = pl.ds(pl.multiple_of(base + begin, 16), end - begin)
        product = contract(cot_ref[...], weight[rows], 1, 1)
        at = pl.ds(pl.multiple_of(base + begin, 128), end - begin)
        slope, act, both = (factor_ref[i, :, at].astype(F32) for i in range(3))
        for k in range(count):
            own = product[k * tokens : (k + 1) * tokens]
            sum_ref[k : k + 1, begin:end] = jnp.sum(own * slope, axis=0, keepdims=True)
            sum_ref[count + k : count + k + 1, begin:end] = jnp.sum(
                own * act, axis=0, keepdims=True
            )
            weighed = own * both
            for lanes in range(0, end - begin, 128):
                stop = min(lanes + 128, end - begin)
                cross[k, :, : stop - lanes] += weighed[:, lanes:stop]

    @pl.when(step < full)
    def _():
        for begin in range(0, BLOCK, 256):
            part(begin, min(begin + 256, BLOCK))

    @pl.when(step == full)
    def _():
        part(0, units - full * BLOCK)

    @pl.when(step == pl.num_programs(0) - 1)
    def _():
        for k in range(count):
            cross_ref[:, k : k + 1] = jnp.sum(cross[k], axis=1, keepdims=True)


def back_product(factor, cot, weight):
    units, width = weight.shape
    tokens = factor.shape[1]
    count = cot.shape[0]
    resident = pl.BlockSpec(memory_space=pltpu.VMEM)
    return pl.pallas_call(
        functools.partial(back_kernel, units),
        grid=(pl.cdiv(units, BLOCK),),
        in_specs=[resident, resident, pl.BlockSpec(memory_space=pltpu.HBM)],
        out_specs=[
            pl.BlockSpec((2 * count, BLOCK), lambda i: (0, i)),
            pl.BlockSpec((tokens, count), lambda i: (0, 0)),
        ],
        out_shape=[
            jax.ShapeDtypeStruct((2 * count, units), F32),
            jax.ShapeDtypeStruct((tokens, count), F32),
        ],
        scratch_shapes=[pltpu.VMEM((count, tokens, 128), F32), *store((weight,))],
        compiler_params=pltpu.CompilerParams(vmem_limit_bytes=52 << 20),
        cost_estimate=pl.CostEstimate(
            flops=2 * count * tokens * units * width,
            bytes_accessed=2 * units * width,
            transcendentals=0,
        ),
        name="back_product",
    )(factor, cot.reshape(count * tokens, width), weight)


def spread(value, axis):
    size = lax.axis_size(axis)
    return lax.all_to_all(jnp.broadcast_to(value[None], (size, *value.shape)), axis, 0, 0)


def gather_row(value, axis, base=0, size=None):
    size = lax.axis_size("row") if size is None else size
    here = lax.axis_index("row") % size
    shape = list(value.shape)
    shape[axis] *= size
    out = jnp.zeros(shape, value.dtype)
    for m in range(size):
        piece = exchange(value, "row", base ^ m) if base ^ m else value
        out = lax.dynamic_update_slice_in_dim(out, piece, (here ^ m) * value.shape[axis], axis=axis)
    return out


def scatter_half(value, rows):
    streams, tokens, width = value.shape
    groups = value.reshape(streams, tokens // rows, rows, width)
    here = lax.axis_index("row")
    mask = 1
    while groups.shape[1] > 1:
        pairs = groups.reshape(streams, groups.shape[1] // 2, 2, rows, width).astype(BF16)
        bit = (here // mask) % 2
        mine = lax.dynamic_index_in_dim(pairs, bit, 2, keepdims=False)
        other = lax.dynamic_index_in_dim(pairs, 1 - bit, 2, keepdims=False)
        groups = mine.astype(F32) + exchange(other, "row", mask).astype(F32)
        mask *= 2
    return groups.reshape(streams, rows, width).astype(F32)


def per_device(hidden, vectors, gain, lengths, gate_weight, up_weight, down_weight):
    rows = hidden.shape[0]
    width = hidden.shape[1]
    count = vectors.shape[0]
    tokens = rows * lax.axis_size("row")
    units = gate_weight.shape[1]
    chunks = lax.axis_size("col")
    per = tokens // chunks
    hidden_all = gather_row(hidden, 0)
    hidden_f = hidden_all.astype(F32)
    scaled_vectors = vectors * gain
    high = scaled_vectors.astype(BF16)
    low = (scaled_vectors - high.astype(F32)).astype(BF16)
    x = jnp.concatenate([(hidden_f * gain).astype(BF16), high, low], axis=0)
    blocks = pl.cdiv(units, BLOCK)
    first = blocks // 2
    mains, vec = products(x, gate_weight.T, up_weight.T, chunks, per, count, first)
    sums = jnp.concatenate(
        [
            jnp.sum(hidden_f * hidden_f, axis=1)[None],
            lax.dot_general(vectors, hidden_f, (((1,), (1,)), ((), ())), precision=HIGH),
        ],
        axis=0,
    )
    arrived, places, vec, sums = ring_sum(
        mains, vec.reshape(2 * count, units), sums.reshape(2 * count, -1)
    )
    vec = vec.reshape(2, count, units)
    sums = sums.reshape(count + 1, tokens)
    scale = lax.rsqrt(sums[:1] / D + EPSILON)
    mix = scale**2 * sums[1:] / D
    row_values = jnp.broadcast_to(
        jnp.concatenate([scale, mix], axis=0)[:, :, None], (count + 1, tokens, 128)
    )
    top = lax.axis_size("row") // 2
    half = tokens // 2
    side = lax.axis_index("row") // top

    def of_half(which):
        return (
            jnp.concatenate([places, which.astype(jnp.int32)[None]]),
            lax.dynamic_slice_in_dim(row_values, which * half, half, axis=1),
        )

    away_places, away_rows = of_half(1 - side)
    source = [piece for part in range(2) for way in range(2) for piece in arrived[part, way]]
    away, away_factor, raw = down_product(
        source, (chunks, per), away_places, vec, away_rows, down_weight, first
    )
    sent = scatter_half(away, rows).astype(BF16)
    got = exchange(sent, "row", top)
    home_places, home_rows = of_half(side)
    home_places, _ = lax.optimization_barrier((home_places, sent))
    home, home_factor = down_product(
        [raw], (chunks, per), home_places, vec, home_rows, down_weight, first
    )
    down = scatter_half(home, rows) + got.astype(F32)
    output = (hidden.astype(F32) + down[0]).astype(BF16)
    tangent = (vectors[:, None] + down[1:]).astype(BF16)
    start = lax.axis_index("row") * rows
    position = start + lax.iota(jnp.int32, rows)
    prompt = position // LEN
    limit = jnp.sum(
        jnp.where(
            prompt[:, None] == lax.iota(jnp.int32, lengths.shape[0])[None, :], lengths[None, :], 0
        ),
        axis=1,
    )
    live = (position % LEN < limit).astype(BF16)
    cotangent = tangent * live[None, :, None]
    home_cot = gather_row(cotangent, 1, 0, top)
    away_cot = gather_row(cotangent, 1, top, top)
    home_sum, home_cross = back_product(home_factor, home_cot, down_weight)
    away_cot, _ = lax.optimization_barrier((away_cot, home_cross))
    away_sum, away_cross = back_product(away_factor, away_cot, down_weight)
    cross_part = jnp.where(
        side == 0,
        jnp.concatenate([home_cross, away_cross], axis=0),
        jnp.concatenate([away_cross, home_cross], axis=0),
    ).T
    rough, exact = home_sum + away_sum, cross_part.reshape(2 * count, -1)
    mask = 1
    while mask < lax.axis_size("col"):
        own = pack(rough, exact)
        mine, theirs = unpack(own, units), unpack(exchange(own, "col", mask), units)
        rough, exact = (x + y for x, y in zip(mine, theirs))
        mask *= 2
    back_sum = rough.astype(BF16)
    cross_part = exact.reshape(count, tokens)
    pulled = gain * (
        contract(back_sum[:count], gate_weight, 1, 1)
        + contract(back_sum[count:], up_weight, 1, 1)
    )
    shift = jnp.dot(cross_part * scale**3 / D, hidden_f, precision=HIGH)
    partial = jnp.sum(cotangent.astype(F32), axis=1) + pulled - shift
    final = doubling(jnp.concatenate([partial, cross_part], axis=1), "row")
    total = final[:, :width]
    back_cross = final[:, width:]
    gram = jnp.sum(spread(jnp.dot(total, total.T, precision=HIGH), "col"), axis=0)
    lower = jnp.linalg.cholesky(gram)
    new_vectors = lax.linalg.triangular_solve(lower, total, left_side=True, lower=True) * D**0.5
    own_cross = lax.dynamic_slice_in_dim(back_cross, start, rows, axis=1).T
    return (output, jnp.transpose(tangent, (1, 0, 2)), new_vectors, own_cross)


def solution(mesh):
    return jax.shard_map(
        per_device,
        mesh=mesh,
        in_specs=(
            P("row", "col"),
            P(None, "col"),
            P("col"),
            P(),
            P("col", "row"),
            P("col", "row"),
            P("row", "col"),
        ),
        out_specs=(P("row", "col"), P("row", None, "col"), P(None, "col"), P("row", None)),
        check_vma=False,
    )
```

```python
import functools

import jax
import jax.numpy as jnp
from jax import lax
from jax.experimental import pallas as pl
from jax.experimental.pallas import tpu as pltpu
from jax.sharding import PartitionSpec as P

D = 8192
LEN = 64


EPSILON = 1e-06
HIGH = lax.Precision.HIGHEST
BLOCK = 896
BF16 = jnp.bfloat16
F32 = jnp.float32


def silu_parts(value):
    sigmoid = jax.nn.sigmoid(value)
    return (value * sigmoid, sigmoid * (1.0 + value * (1.0 - sigmoid)))


def contract(left, right, left_dim, right_dim):
    return lax.dot_general(
        left, right, (((left_dim,), (right_dim,)), ((), ())), preferred_element_type=jnp.float32
    )


def exchange(value, axis, mask):
    size = lax.axis_size(axis)
    return lax.ppermute(value, axis, [(i, i ^ mask) for i in range(size)])


def doubling(value, axis, send=None):
    mask = 1
    while mask < lax.axis_size(axis):
        if send is None:
            value = jax.tree.map(lambda v: v + exchange(v, axis, mask), value)
        else:
            own = value.astype(send)
            value = own.astype(F32) + exchange(own, axis, mask).astype(F32)
        mask *= 2
    return value


def starts(units):
    return [(begin, min(BLOCK, units - begin)) for begin in range(0, units, BLOCK)]


def fetch(sources, copies, arrived):
    def copy(which, block, begin, size):
        rows = pl.ds(begin, size)
        return pltpu.make_async_copy(
            sources[which].at[rows], copies[which].at[rows], arrived.at[which, block]
        )

    blocks = starts(sources[0].shape[0])
    step = pl.program_id(0)

    @pl.when(step == 0)
    def _():
        for block, place in enumerate(blocks):
            for which in range(len(sources)):
                copy(which, block, *place).start()

    def wait(block, last=False):
        for which in range(len(sources)):
            if last:
                copy(which, len(blocks) - 1, *blocks[-1]).wait()
            else:
                copy(which, block, pl.multiple_of(block * BLOCK, BLOCK), BLOCK).wait()

    return wait


def store(weights):
    units, width = weights[0].shape
    return [pltpu.VMEM((units, width), BF16) for _ in weights] + [
        pltpu.SemaphoreType.DMA((len(weights), pl.cdiv(units, BLOCK)))
    ]


def products_kernel(first, x_ref, gate_hbm, up_hbm, *refs):
    outs = (refs[0:2], refs[2:4])
    vec_ref, *weights, arrived = refs[4:]
    wait = fetch((gate_hbm, up_hbm), weights, arrived)
    step = pl.program_id(0)
    chunks, per, _ = outs[0][0].shape
    count = vec_ref.shape[1]
    tokens = chunks * per
    units = vec_ref.shape[2]
    full = units // BLOCK

    def put(part, begin, size):
        at = pl.ds(pl.multiple_of((step - begin) * BLOCK, 128), size)
        to = pl.ds(pl.multiple_of(step * BLOCK, 128), size)
        for index in range(2):
            weight = weights[index][pl.ds(pl.multiple_of(step * BLOCK, BLOCK), size)]
            result = contract(weight, x_ref[...], 1, 1).T
            outs[part][index][:, :, at] = result[:tokens].reshape(chunks, per, size).astype(BF16)
            vec_ref[index, :, to] = result[tokens : tokens + count] + result[tokens + count :]

    pl.when(step < full)(lambda: wait(step))
    pl.when(step == full)(lambda: wait(step, True))
    pl.when(step < first)(lambda: put(0, 0, BLOCK))
    pl.when(jnp.logical_and(step >= first, step < full))(lambda: put(1, first, BLOCK))
    pl.when(step == full)(lambda: put(1, first, units - full * BLOCK))


def products(x, gate_turned, up_turned, chunks, per, count, first):
    units, depth = gate_turned.shape
    resident = pl.BlockSpec(memory_space=pltpu.VMEM)
    anywhere = pl.BlockSpec(memory_space=pltpu.HBM)
    part = lambda width: jax.ShapeDtypeStruct((chunks, per, width), BF16)
    widths = (first * BLOCK, units - first * BLOCK)
    *mains, vec = pl.pallas_call(
        functools.partial(products_kernel, first),
        grid=(units // BLOCK + 1,),
        in_specs=[resident, anywhere, anywhere],
        out_specs=[resident] * 5,
        out_shape=[part(width) for width in widths for _ in range(2)]
        + [jax.ShapeDtypeStruct((2, count, units), F32)],
        scratch_shapes=store((gate_turned, up_turned)),
        compiler_params=pltpu.CompilerParams(vmem_limit_bytes=40 << 20),
        cost_estimate=pl.CostEstimate(
            flops=4 * x.shape[0] * depth * units,
            bytes_accessed=4 * depth * units,
            transcendentals=0,
        ),
        name="products",
    )(x, gate_turned, up_turned)
    return [mains[:2], mains[2:]], vec


def halves(value):
    high = value.astype(BF16)
    return [high, (value - high.astype(F32)).astype(BF16)]


def pack(rough, exact):
    return jnp.concatenate([rough.astype(BF16), *halves(exact)], axis=1)


def unpack(packed, width):
    wide = packed.astype(F32)
    size = (packed.shape[1] - width) // 2
    return wide[:, :width], wide[:, width : width + size] + wide[:, width + size :]


def ring_sum(mains, rough, exact):
    size = lax.axis_size("col")
    order = list(range(0, size, 2)) + list(range(1, size, 2))[::-1]
    column = lax.axis_index("col")
    place = jnp.where(column % 2 == 0, column // 2, size - 1 - column // 2)
    perms = (
        [(order[i], order[(i + 1) % size]) for i in range(size)],
        [(order[(i + 1) % size], order[i]) for i in range(size)],
    )
    signs = (-1, 1)
    streams = [(part, way) for part in range(len(mains)) for way in range(2)]

    def slot(way, offset):
        return (place + signs[way] * offset + size) % size

    def chunk(stream, offset):
        part, way = stream
        return lax.dynamic_index_in_dim(mains[part][way], slot(way, offset), 0, keepdims=False)

    flight = {"rough": rough, "exact": exact, "mask": 1, "count": 0}

    def side(mark):
        count = flight["count"]
        flight["count"] += 1
        if count < 4:
            return
        if (count - 4) % 3 == 0 and flight["mask"] < size:
            own, _ = lax.optimization_barrier((pack(flight["rough"], flight["exact"]), mark))
            flight["pair"] = (own, exchange(own, "col", flight["mask"]))
            flight["mask"] *= 2
        elif (count - 4) % 3 == 2 and "pair" in flight:
            own, other = flight.pop("pair")
            other, _ = lax.optimization_barrier((other, mark))
            width = rough.shape[1]
            mine, theirs = unpack(own, width), unpack(other, width)
            flight["rough"], flight["exact"] = (x + y for x, y in zip(mine, theirs))

    held = {s: chunk(s, 1) for s in streams}
    for step in range(size - 1):
        for s in streams:
            got = lax.ppermute(held[s], "col", perms[s[1]])
            held[s] = (got.astype(F32) + chunk(s, step + 2).astype(F32)).astype(BF16)
        side(held[streams[-1]])
    arrived = {s: [held[s]] for s in streams}
    for step in range(size - 1):
        for s in streams:
            arrived[s].append(lax.ppermute(arrived[s][-1], "col", perms[s[1]]))
        side(arrived[streams[-1]][-1])
    places = jnp.stack([slot(way, offset) for way in range(2) for offset in range(size)])
    return arrived, places.astype(jnp.int32), flight["rough"], flight["exact"]


def down_kernel(first, full, chunks, collecting, places, *refs):
    if collecting:
        arrived, refs = refs[: 4 * chunks], refs[4 * chunks :]
        vec_ref, rows_ref, hbm, out_ref, factor_ref, raw, held, acc, weight, ready = refs
    else:
        raw, vec_ref, rows_ref, hbm, out_ref, factor_ref, held, acc, weight, ready = refs
    step = pl.program_id(0)
    streams, tokens, width = out_ref.shape
    per = raw.shape[2]
    tail = weight.shape[0] - full * BLOCK
    wait = fetch((hbm,), (weight,), ready)
    group = max(1, 16 // per)
    half = places[2 * chunks] * (chunks // 2)

    def collect(part, at, to):
        for way in range(2):
            for index in range(chunks):
                piece = arrived[(2 * part + way) * chunks + index]
                raw[way, places[way * chunks + index], :, to] = piece[:, at]

    def lanes(block):
        return pl.ds(pl.multiple_of(block * BLOCK, 128), BLOCK)

    if collecting:

        @pl.when(step < first)
        def _():
            collect(0, lanes(step), lanes(step))

        @pl.when(jnp.logical_and(step >= first, step < full))
        def _():
            collect(1, lanes(step - first), lanes(step))

        @pl.when(step == full)
        def _():
            begin = (full - first) * BLOCK
            collect(1, slice(begin, begin + tail), slice(full * BLOCK, full * BLOCK + tail))

    def fill(slot, number, lane):
        size = group * per
        rows = slice(number * size, (number + 1) * size)
        chosen = pl.ds(half + number * group, group)
        here = slice(lane, lane + 128)
        at = pl.ds(pl.multiple_of(step * BLOCK + lane, 128), 128)
        gate_raw, up_raw = (
            raw[way, chosen, :, at].astype(F32).reshape(size, 128) for way in range(2)
        )
        scale = rows_ref[0, rows]
        gate = gate_raw * scale
        up = up_raw * scale
        act, slope = silu_parts(gate)
        slope_up = slope * up
        primal = act * up
        both = slope_up * gate + primal
        scaled_slope = slope_up * scale
        scaled_act = act * scale
        factor_ref[0, rows, at] = scaled_slope.astype(BF16)
        factor_ref[1, rows, at] = scaled_act.astype(BF16)
        factor_ref[2, rows, at] = (slope_up * gate_raw + act * up_raw).astype(BF16)
        held[slot, 0, rows, here] = primal.astype(BF16)
        for k in range(streams - 1):
            held[slot, k + 1, rows, here] = (
                scaled_slope * vec_ref[0, k : k + 1, here]
                + scaled_act * vec_ref[1, k : k + 1, here]
                - rows_ref[k + 1, rows] * both
            ).astype(BF16)

    def last():
        return held[1 - step % 2].reshape(streams * tokens, BLOCK)

    def fill_all():
        for number in range(tokens // (group * per)):
            for lane in range(0, BLOCK, 128):
                fill(step % 2, number, lane)

    @pl.when(step == 0)
    def _():
        acc[...] = jnp.zeros_like(acc)
        fill_all()

    @pl.when(jnp.logical_and(step >= 1, step <= full))
    def _():
        wait(step - 1)
        rows = pl.ds(pl.multiple_of((step - 1) * BLOCK, BLOCK), BLOCK)
        acc[...] += jnp.dot(last(), weight[rows], preferred_element_type=F32)
        fill_all()

    @pl.when(step == full + 1)
    def _():
        wait(full, True)
        rows = slice(full * BLOCK, full * BLOCK + tail)
        result = acc[...] + jnp.dot(last()[:, :tail], weight[rows], preferred_element_type=F32)
        out_ref[...] = result.reshape(streams, tokens, width).astype(BF16)


def down_product(source, shape, places, vec, row_values, weight, first):
    units, width = weight.shape
    full = units // BLOCK
    chunks, per = shape
    tokens = row_values.shape[1]
    count = vec.shape[1]
    resident = pl.BlockSpec(memory_space=pltpu.VMEM)
    padded = (full + 1) * BLOCK
    collecting = len(source) > 1
    return pl.pallas_call(
        functools.partial(down_kernel, first, full, chunks, collecting),
        grid_spec=pltpu.PrefetchScalarGridSpec(
            num_scalar_prefetch=1,
            grid=(full + 2,),
            in_specs=[resident] * len(source)
            + [
                pl.BlockSpec((2, count, BLOCK), lambda i, p: (0, 0, jnp.minimum(i, full))),
                resident,
                pl.BlockSpec(memory_space=pltpu.HBM),
            ],
            out_specs=[
                pl.BlockSpec((count + 1, tokens, width), lambda i, p: (0, 0, 0)),
                resident,
            ]
            + [resident] * collecting,
            scratch_shapes=[
                pltpu.VMEM((2, count + 1, tokens, BLOCK), BF16),
                pltpu.VMEM(((count + 1) * tokens, width), F32),
                *store((weight,)),
            ],
        ),
        out_shape=[
            jax.ShapeDtypeStruct((count + 1, tokens, width), BF16),
            jax.ShapeDtypeStruct((3, tokens, padded), BF16),
        ]
        + [jax.ShapeDtypeStruct((2, chunks, per, padded), BF16)] * collecting,
        compiler_params=pltpu.CompilerParams(vmem_limit_bytes=(46 if collecting else 48) << 20),
        cost_estimate=pl.CostEstimate(
            flops=2 * (count + 1) * tokens * units * width,
            bytes_accessed=2 * units * width,
            transcendentals=tokens * units,
        ),
        name="down_product",
    )(places, *source, vec, row_values, weight)


def back_kernel(units, factor_ref, cot_ref, hbm, sum_ref, cross_ref, cross, weight, ready):
    step = pl.program_id(0)
    tokens = factor_ref.shape[1]
    count = cot_ref.shape[0] // tokens
    base = step * BLOCK

    @pl.when(step == 0)
    def _():
        cross[...] = jnp.zeros_like(cross)

    full = units // BLOCK
    wait = fetch((hbm,), (weight,), ready)
    pl.when(step < full)(lambda: wait(step))
    pl.when(step == full)(lambda: wait(step, True))

    def part(begin, end):
        rows = pl.ds(pl.multiple_of(base + begin, 16), end - begin)
        product = contract(cot_ref[...], weight[rows], 1, 1)
        at = pl.ds(pl.multiple_of(base + begin, 128), end - begin)
        slope, act, both = (factor_ref[i, :, at].astype(F32) for i in range(3))
        for k in range(count):
            own = product[k * tokens : (k + 1) * tokens]
            sum_ref[k : k + 1, begin:end] = jnp.sum(own * slope, axis=0, keepdims=True)
            sum_ref[count + k : count + k + 1, begin:end] = jnp.sum(
                own * act, axis=0, keepdims=True
            )
            weighed = own * both
            for lanes in range(0, end - begin, 128):
                stop = min(lanes + 128, end - begin)
                cross[k, :, : stop - lanes] += weighed[:, lanes:stop]

    @pl.when(step < full)
    def _():
        for begin in range(0, BLOCK, 256):
            part(begin, min(begin + 256, BLOCK))

    @pl.when(step == full)
    def _():
        part(0, units - full * BLOCK)

    @pl.when(step == pl.num_programs(0) - 1)
    def _():
        for k in range(count):
            cross_ref[:, k : k + 1] = jnp.sum(cross[k], axis=1, keepdims=True)


def back_product(factor, cot, weight):
    units, width = weight.shape
    tokens = factor.shape[1]
    count = cot.shape[0]
    resident = pl.BlockSpec(memory_space=pltpu.VMEM)
    return pl.pallas_call(
        functools.partial(back_kernel, units),
        grid=(pl.cdiv(units, BLOCK),),
        in_specs=[resident, resident, pl.BlockSpec(memory_space=pltpu.HBM)],
        out_specs=[
            pl.BlockSpec((2 * count, BLOCK), lambda i: (0, i)),
            pl.BlockSpec((tokens, count), lambda i: (0, 0)),
        ],
        out_shape=[
            jax.ShapeDtypeStruct((2 * count, units), F32),
            jax.ShapeDtypeStruct((tokens, count), F32),
        ],
        scratch_shapes=[pltpu.VMEM((count, tokens, 128), F32), *store((weight,))],
        compiler_params=pltpu.CompilerParams(vmem_limit_bytes=52 << 20),
        cost_estimate=pl.CostEstimate(
            flops=2 * count * tokens * units * width,
            bytes_accessed=2 * units * width,
            transcendentals=0,
        ),
        name="back_product",
    )(factor, cot.reshape(count * tokens, width), weight)


def spread(value, axis):
    size = lax.axis_size(axis)
    return lax.all_to_all(jnp.broadcast_to(value[None], (size, *value.shape)), axis, 0, 0)


def gather_row(value, axis, base=0, size=None):
    size = lax.axis_size("row") if size is None else size
    here = lax.axis_index("row") % size
    shape = list(value.shape)
    shape[axis] *= size
    out = jnp.zeros(shape, value.dtype)
    for m in range(size):
        piece = exchange(value, "row", base ^ m) if base ^ m else value
        out = lax.dynamic_update_slice_in_dim(out, piece, (here ^ m) * value.shape[axis], axis=axis)
    return out


def scatter_half(value, rows):
    streams, tokens, width = value.shape
    groups = value.reshape(streams, tokens // rows, rows, width)
    here = lax.axis_index("row")
    mask = 1
    while groups.shape[1] > 1:
        pairs = groups.reshape(streams, groups.shape[1] // 2, 2, rows, width).astype(BF16)
        bit = (here // mask) % 2
        mine = lax.dynamic_index_in_dim(pairs, bit, 2, keepdims=False)
        other = lax.dynamic_index_in_dim(pairs, 1 - bit, 2, keepdims=False)
        groups = mine.astype(F32) + exchange(other, "row", mask).astype(F32)
        mask *= 2
    return groups.reshape(streams, rows, width).astype(F32)


def per_device(hidden, vectors, gain, lengths, gate_weight, up_weight, down_weight):
    rows = hidden.shape[0]
    width = hidden.shape[1]
    count = vectors.shape[0]
    tokens = rows * lax.axis_size("row")
    units = gate_weight.shape[1]
    chunks = lax.axis_size("col")
    per = tokens // chunks
    hidden_all = gather_row(hidden, 0)
    hidden_f = hidden_all.astype(F32)
    scaled_vectors = vectors * gain
    high = scaled_vectors.astype(BF16)
    low = (scaled_vectors - high.astype(F32)).astype(BF16)
    x = jnp.concatenate([(hidden_f * gain).astype(BF16), high, low], axis=0)
    blocks = pl.cdiv(units, BLOCK)
    first = blocks // 2
    mains, vec = products(x, gate_weight.T, up_weight.T, chunks, per, count, first)
    sums = jnp.concatenate(
        [
            jnp.sum(hidden_f * hidden_f, axis=1)[None],
            lax.dot_general(vectors, hidden_f, (((1,), (1,)), ((), ())), precision=HIGH),
        ],
        axis=0,
    )
    arrived, places, vec, sums = ring_sum(
        mains, vec.reshape(2 * count, units), sums.reshape(2 * count, -1)
    )
    vec = vec.reshape(2, count, units)
    sums = sums.reshape(count + 1, tokens)
    scale = lax.rsqrt(sums[:1] / D + EPSILON)
    mix = scale**2 * sums[1:] / D
    row_values = jnp.broadcast_to(
        jnp.concatenate([scale, mix], axis=0)[:, :, None], (count + 1, tokens, 128)
    )
    top = lax.axis_size("row") // 2
    half = tokens // 2
    side = lax.axis_index("row") // top

    def of_half(which):
        return (
            jnp.concatenate([places, which.astype(jnp.int32)[None]]),
            lax.dynamic_slice_in_dim(row_values, which * half, half, axis=1),
        )

    away_places, away_rows = of_half(1 - side)
    source = [piece for part in range(2) for way in range(2) for piece in arrived[part, way]]
    away, away_factor, raw = down_product(
        source, (chunks, per), away_places, vec, away_rows, down_weight, first
    )
    sent = scatter_half(away, rows).astype(BF16)
    got = exchange(sent, "row", top)
    home_places, home_rows = of_half(side)
    home_places, _ = lax.optimization_barrier((home_places, sent))
    home, home_factor = down_product(
        [raw], (chunks, per), home_places, vec, home_rows, down_weight, first
    )
    down = scatter_half(home, rows) + got.astype(F32)
    output = (hidden.astype(F32) + down[0]).astype(BF16)
    tangent = (vectors[:, None] + down[1:]).astype(BF16)
    start = lax.axis_index("row") * rows
    position = start + lax.iota(jnp.int32, rows)
    prompt = position // LEN
    limit = jnp.sum(
        jnp.where(
            prompt[:, None] == lax.iota(jnp.int32, lengths.shape[0])[None, :], lengths[None, :], 0
        ),
        axis=1,
    )
    live = (position % LEN < limit).astype(BF16)
    cotangent = tangent * live[None, :, None]
    home_cot = gather_row(cotangent, 1, 0, top)
    away_cot = gather_row(cotangent, 1, top, top)
    home_sum, home_cross = back_product(home_factor, home_cot, down_weight)
    away_cot, _ = lax.optimization_barrier((away_cot, home_cross))
    away_sum, away_cross = back_product(away_factor, away_cot, down_weight)
    cross_part = jnp.where(
        side == 0,
        jnp.concatenate([home_cross, away_cross], axis=0),
        jnp.concatenate([away_cross, home_cross], axis=0),
    ).T
    rough, exact = home_sum + away_sum, cross_part.reshape(2 * count, -1)
    mask = 1
    while mask < lax.axis_size("col"):
        own = pack(rough, exact)
        mine, theirs = unpack(own, units), unpack(exchange(own, "col", mask), units)
        rough, exact = (x + y for x, y in zip(mine, theirs))
        mask *= 2
    back_sum = rough.astype(BF16)
    cross_part = exact.reshape(count, tokens)
    pulled = gain * (
        contract(back_sum[:count], gate_weight, 1, 1)
        + contract(back_sum[count:], up_weight, 1, 1)
    )
    shift = jnp.dot(cross_part * scale**3 / D, hidden_f, precision=HIGH)
    partial = jnp.sum(cotangent.astype(F32), axis=1) + pulled - shift
    final = doubling(jnp.concatenate([partial, cross_part], axis=1), "row")
    total = final[:, :width]
    back_cross = final[:, width:]
    gram = jnp.sum(spread(jnp.dot(total, total.T, precision=HIGH), "col"), axis=0)
    lower = jnp.linalg.cholesky(gram)
    new_vectors = lax.linalg.triangular_solve(lower, total, left_side=True, lower=True) * D**0.5
    own_cross = lax.dynamic_slice_in_dim(back_cross, start, rows, axis=1).T
    return (output, jnp.transpose(tangent, (1, 0, 2)), new_vectors, own_cross)


def solution(mesh):
    return jax.shard_map(
        per_device,
        mesh=mesh,
        in_specs=(
            P("row", "col"),
            P(None, "col"),
            P("col"),
            P(),
            P("col", "row"),
            P("col", "row"),
            P("row", "col"),
        ),
        out_specs=(P("row", "col"), P("row", None, "col"), P(None, "col"), P("row", None)),
        check_vma=False,
    )
```
